128 devices in a mesh: tm: 8 (over z_hi, x), space: 16 (over z_lo, y, core).
Axes of the slice: x: 4, y: 4, z: 4 (z_hi: 2, z_lo: 2; z = z_hi * 2 + z_lo), core: 2. Of those that a mesh axis runs over, the one named last changes fastest.
Arguments:
- activations: bfloat16 [64, 32, 8, 1024], P('tm', 'space'), may hold values from -6 to 6
- in_proj: bfloat16 [1024, 2176], replicated, may hold values from -0.1875 to 0.1875
- step_proj: bfloat16 [1024, 16], replicated, may hold values from -0.1875 to 0.1875
- step_bias: float32 [16], replicated, may hold values from -2 to 0
- decay_rates: float32 [16], replicated, may hold values from 0.005 to 0.5
- conv_kernel: float32 [3, 3, 1152], replicated, may hold values from -2 to 2
- conv_bias: float32 [1152], replicated, may hold values from -3 to 3
- skip_gain: float32 [16], replicated, may hold values from 0.5 to 1.5
- norm_gain: float32 [1024], replicated, may hold values from 0.5 to 1.5
- out_proj: bfloat16 [1024, 1024], replicated, may hold values from -0.1875 to 0.1875
- out_cotangent: bfloat16 [64, 32, 8, 1024], P('tm', 'space'), may hold values from -6 to 6
Outputs:
- layer_out: bfloat16 [64, 32, 8, 1024], P('tm', 'space')
- grad_input: bfloat16 [64, 32, 8, 1024], P('tm', 'space')
- grad_in_proj: float32 [1024, 2176], P(('tm', 'space'))
- grad_step_proj: float32 [1024, 16], P(('tm', 'space'))
- grad_out_proj_t: float32 [1024, 1024], P(('tm', 'space'))
- grad_conv_kernel: float32 [3, 3, 1152], replicated
- grad_conv_bias: float32 [1152], replicated
- grad_step_bias: float32 [16], replicated
- grad_decay_rates: float32 [16], replicated
- grad_skip_gain: float32 [16], replicated
- grad_norm_gain: float32 [1024], replicated
The draws below stay inside these ranges and needn't reach their ends.
All inputs are finite; a program needn't handle non-finite values.
Results may differ from the reference program's by a relative error of at most 0.015.
The reference program's roundings to bfloat16 on the way (of `gate_z`, `mixed_in`, `step_sizes`, `activated`, `ssd_out`, `normed` and `d_projected`) count: a program that leaves them out, or rounds other values in their place, can miss the bound.
Values may be sent and summed in bfloat16 or wider, within the bound.
No kernel may reach another device: no remote copies, remote signals or barrier semaphores. Data moves between devices by JAX's collectives and lax.ppermute only.
A program may use at most 192 MiB of HBM per device.

```python
import math
import jax
import jax.numpy as jnp
from jax import lax

D = 1024
HEADS = 16
COLS = 8
FR_DEV = 8
EI = 1024
XC = 1152
FRAMES = 64
ROWS = 32


def strengthened(drawn, rng, source, target, shards_of, factor):
    owner, partner = [(jnp.arange(drawn.shape[position]) // (drawn.shape[position] // shards_of)).reshape([-1 if axis == position else 1 for axis in range(drawn.ndim)]) for position in (source, target)]
    chosen = jax.random.permutation(rng, shards_of)[partner]
    strong = (owner == chosen) | (owner == (partner + shards_of // 2) % shards_of)
    return jnp.where(strong, factor * drawn, drawn)


def level_of(key, extent, cuts, least, largest):
    def one(position, blocks):
        heights = jax.random.uniform(jax.random.fold_in(jax.random.fold_in(key, 6), position), (blocks,), jnp.float32, least / len(cuts), largest / len(cuts))
        return jnp.repeat(jnp.exp(heights), extent[position] // blocks).reshape((-1,) + (1,) * (len(extent) - position - 1))

    level = one(*cuts[0])
    for cut in cuts[1:]:
        level = level * one(*cut)
    return level


def noise(key, dims, deviation, most, shards=(), held_as=jnp.bfloat16):
    values = deviation * jax.random.normal(key, dims, jnp.float32)
    if shards:
        values = values * level_of(key, dims, shards, -0.22, 0.18)
    return jnp.clip(values, -most, most).astype(held_as)


def noise_with(own_key, dims, deviation, most, split, heavy, held_as=jnp.bfloat16):
    entries = deviation * jax.random.normal(own_key, dims, jnp.float32)
    if split:
        entries = entries * level_of(own_key, dims, split, -0.22, 0.18)
    return jnp.clip(strengthened(entries, jax.random.fold_in(own_key, 3), *heavy), -most, most).astype(held_as)


def setup_inputs(seed: int = 0) -> dict:
    arg_keys = jax.random.split(jax.random.key(seed), 12)
    activations = noise_with(arg_keys[0], (FRAMES, ROWS, COLS, D), 1.0, 6.0, ((0, 8), (1, 16)), (0, 3, 8, 2.0))
    in_proj = noise(arg_keys[1], (D, EI + XC), D ** -0.5, 0.1875)
    step_proj = noise(arg_keys[2], (D, HEADS), D ** -0.5, 0.1875)
    step_bias = jnp.clip(jax.random.uniform(arg_keys[3], (HEADS,), jnp.float32, -2.0, 0.0), -2.0, 0.0)
    decay_rates = jnp.clip(jnp.exp(jax.random.uniform(arg_keys[4], (HEADS,), jnp.float32, math.log(0.005), math.log(0.5))), 0.005, 0.5)
    conv_kernel = noise(arg_keys[5], (3, 3, XC), 9 ** -0.5, 2.0, (), jnp.float32)
    conv_bias = noise(arg_keys[6], (XC,), 0.5, 3.0, (), jnp.float32)
    skip_gain = jnp.clip(jax.random.uniform(arg_keys[7], (HEADS,), jnp.float32, 0.5, 1.5), 0.5, 1.5)
    norm_gain = jnp.clip(1.0 + 0.1 * jax.random.normal(arg_keys[8], (EI,), jnp.float32), 0.5, 1.5)
    out_proj = noise(arg_keys[9], (EI, D), EI ** -0.5, 0.1875)
    out_cotangent = noise_with(arg_keys[10], (FRAMES, ROWS, COLS, D), 1.0, 6.0, ((0, 8), (1, 16)), (1, 3, 16, 2.0))
    return dict(activations=activations, in_proj=in_proj, step_proj=step_proj, step_bias=step_bias, decay_rates=decay_rates, conv_kernel=conv_kernel, conv_bias=conv_bias, skip_gain=skip_gain, norm_gain=norm_gain, out_proj=out_proj, out_cotangent=out_cotangent)


top_precision = lax.Precision.HIGHEST
norm_eps = 1e-05

def ssd_block(heads_in, b_proj, c_proj, step_in, rate_in, gain_in, state_in):
    decay_step = step_in * rate_in
    running = jnp.cumsum(decay_step, axis=0)
    places = jnp.arange(heads_in.shape[0])
    causal = (places[:, None] >= places[None, :])[:, :, None, None]
    spread = running[:, None] - running[None, :]
    weights = jnp.where(causal, jnp.exp(-jnp.where(causal, spread, 0.0)), 0.0) * step_in[None, :]
    inner_cb = jnp.einsum('tkn,skn->tsk', c_proj, b_proj, precision=top_precision)
    intra_part = jnp.einsum('tskh,skhp->tkhp', weights * inner_cb[..., None], heads_in, precision=top_precision)
    carried = jnp.exp(-running)[..., None] * jnp.einsum('tkn,khpn->tkhp', c_proj, state_in, precision=top_precision)
    result = intra_part + carried + gain_in[:, None] * heads_in
    final_sum = running[-1]
    tail_weight = jnp.exp(running - final_sum[None]) * step_in
    state_out = jnp.exp(-final_sum)[..., None, None] * state_in + jnp.einsum('skh,skhp,skn->khpn', tail_weight, heads_in, b_proj, precision=top_precision)
    return (result, state_out)

def ssd_sequence(heads_in, b_proj, c_proj, step_in, rate_in, gain_in, block_len):
    block_count = heads_in.shape[0] // block_len

    def fold_blocks(array_in):
        return array_in.reshape((block_count, block_len) + array_in.shape[1:])
    start_state = jnp.zeros(heads_in.shape[1:4] + (b_proj.shape[2],), jnp.float32)

    def advance(carry_state, pieces):
        result, carry_state = ssd_block(pieces[0], pieces[1], pieces[2], pieces[3], rate_in, gain_in, carry_state)
        return (carry_state, result)
    final_state, results = lax.scan(advance, start_state, (fold_blocks(heads_in), fold_blocks(b_proj), fold_blocks(c_proj), fold_blocks(step_in)))
    return (results.reshape(heads_in.shape), final_state)

def gate_norm(ssd_float, gate_float, norm_gain):
    gated = ssd_float * jax.nn.silu(gate_float)
    scale_row = lax.rsqrt(lax.optimization_barrier(jnp.mean(gated * gated, axis=-1, keepdims=True)) + norm_eps)
    return gated * scale_row * norm_gain

def silu_slope(before):
    squashed = jax.nn.sigmoid(before)
    return squashed * (1.0 + before * (1.0 - squashed))

def conv_apply(padded, conv_kernel, conv_bias, row_count, col_count):
    accum = conv_kernel[0, 0] * padded[:, 0:row_count, 0:col_count]
    for row_off in range(3):
        for col_off in range(3):
            if row_off + col_off > 0:
                accum = accum + conv_kernel[row_off, col_off] * padded[:, row_off:row_off + row_count, col_off:col_off + col_count]
    return accum + conv_bias

def conv_transpose(d_padded, conv_kernel, row_count, col_count):
    accum = conv_kernel[0, 0] * d_padded[:, 2:2 + row_count, 2:2 + col_count]
    for row_off in range(3):
        for col_off in range(3):
            if row_off + col_off > 0:
                accum = accum + conv_kernel[row_off, col_off] * d_padded[:, 2 - row_off:2 - row_off + row_count, 2 - col_off:2 - col_off + col_count]
    return accum

def kernel_grad(d_before, padded, row_count, col_count):
    parts = []
    for row_off in range(3):
        for col_off in range(3):
            parts.append(lax.optimization_barrier(jnp.sum(d_before * padded[:, row_off:row_off + row_count, col_off:col_off + col_count], axis=(0, 1, 2))))
    return jnp.stack(parts).reshape(3, 3, -1)

def reference(activations, in_proj, step_proj, step_bias, decay_rates, conv_kernel, conv_bias, skip_gain, norm_gain, out_proj, out_cotangent):
    frame_count, row_count, col_count, model_width = activations.shape
    inner_w = out_proj.shape[0]
    head_count = step_proj.shape[1]
    head_dim = inner_w // head_count
    state_n = (in_proj.shape[1] - 2 * inner_w) // 2
    flat_act = activations.reshape(-1, model_width)
    projected = jnp.dot(flat_act, in_proj, preferred_element_type=jnp.float32)
    gate_z = projected[:, :inner_w].astype(jnp.bfloat16)
    mixed_in = projected[:, inner_w:].astype(jnp.bfloat16).reshape(frame_count, row_count, col_count, -1)
    step_raw = jnp.dot(flat_act, step_proj, preferred_element_type=jnp.float32) + step_bias
    step_sizes = jax.nn.softplus(step_raw).astype(jnp.bfloat16)
    padded = jnp.pad(mixed_in.astype(jnp.float32), ((0, 0), (1, 1), (1, 1), (0, 0)))
    before = conv_apply(padded, conv_kernel, conv_bias, row_count, col_count)
    activated = jax.nn.silu(before).astype(jnp.bfloat16)
    per_row = jnp.transpose(activated, (1, 0, 2, 3))
    steps_row = jnp.transpose(step_sizes.reshape(frame_count, row_count, col_count, head_count), (1, 0, 2, 3))

    def split_row(row_act):
        act_float = row_act.astype(jnp.float32)
        heads_in = act_float[..., :inner_w].reshape(frame_count, col_count, head_count, head_dim)
        return (heads_in, act_float[..., inner_w:inner_w + state_n], act_float[..., inner_w + state_n:])

    def forward_row(pieces):
        heads_in, b_proj, c_proj = split_row(pieces[0])
        result, _ = ssd_sequence(heads_in, b_proj, c_proj, pieces[1].astype(jnp.float32), decay_rates, skip_gain, FR_DEV)
        return result.astype(jnp.bfloat16)
    ssd_rows = lax.map(forward_row, (per_row, steps_row))
    ssd_out = jnp.transpose(ssd_rows, (1, 0, 2, 3, 4)).reshape(-1, inner_w)
    normed = gate_norm(ssd_out.astype(jnp.float32), gate_z.astype(jnp.float32), norm_gain).astype(jnp.bfloat16)
    layer_out = jnp.dot(normed, out_proj, preferred_element_type=jnp.float32).astype(jnp.bfloat16).reshape(activations.shape)
    contract_rows = (((0,), (0,)), ((), ()))
    contract_cols = (((1,), (1,)), ((), ()))
    cot_flat = out_cotangent.reshape(-1, model_width)
    d_normed = lax.dot_general(cot_flat, out_proj, contract_cols, preferred_element_type=jnp.float32)
    grad_out_proj_t = lax.dot_general(cot_flat, normed, contract_rows, preferred_element_type=jnp.float32)
    _, pull_norm = jax.vjp(gate_norm, ssd_out.astype(jnp.float32), gate_z.astype(jnp.float32), norm_gain)
    d_ssd, d_gate, grad_norm_gain = pull_norm(d_normed)
    d_ssd = d_ssd.astype(jnp.bfloat16)
    d_rows = jnp.transpose(d_ssd.reshape(frame_count, row_count, col_count, head_count, head_dim), (1, 0, 2, 3, 4))

    def backward_row(pieces):

        def ssd_local(heads_in, b_proj, c_proj, step_in, rate_in, gain_in):
            return ssd_sequence(heads_in, b_proj, c_proj, step_in, rate_in, gain_in, FR_DEV)
        heads_in, b_proj, c_proj = split_row(pieces[0])
        outputs, pull_back = jax.vjp(ssd_local, heads_in, b_proj, c_proj, pieces[1].astype(jnp.float32), decay_rates, skip_gain)
        gradients = pull_back((pieces[2].astype(jnp.float32), jnp.zeros_like(outputs[1])))
        d_act = jnp.concatenate([gradients[0].reshape(frame_count, col_count, inner_w), gradients[1], gradients[2]], axis=-1).astype(jnp.bfloat16)
        return (d_act, gradients[3].astype(jnp.bfloat16), gradients[4], gradients[5])
    d_act_rows, d_step_rows, rate_parts, gain_parts = lax.map(backward_row, (per_row, steps_row, d_rows))
    grad_decay_rates = lax.optimization_barrier(jnp.sum(rate_parts, axis=0))
    grad_skip_gain = lax.optimization_barrier(jnp.sum(gain_parts, axis=0))
    d_act = jnp.transpose(d_act_rows, (1, 0, 2, 3)).astype(jnp.float32)
    d_before = d_act * silu_slope(before)
    grad_conv_kernel = kernel_grad(d_before, padded, row_count, col_count)
    grad_conv_bias = lax.optimization_barrier(jnp.sum(d_before, axis=(0, 1, 2)))
    d_padded = jnp.pad(d_before, ((0, 0), (1, 1), (1, 1), (0, 0)))
    d_mixed = conv_transpose(d_padded, conv_kernel, row_count, col_count)
    d_steps = jnp.transpose(d_step_rows, (1, 0, 2, 3)).reshape(-1, head_count).astype(jnp.float32)
    d_raw = d_steps * jax.nn.sigmoid(step_raw)
    grad_step_bias = lax.optimization_barrier(jnp.sum(d_raw, axis=0))
    d_raw_half = d_raw.astype(jnp.bfloat16)
    d_projected = jnp.concatenate([d_gate, d_mixed.reshape(-1, d_mixed.shape[-1])], axis=1).astype(jnp.bfloat16)
    grad_input = (lax.dot_general(d_projected, in_proj, contract_cols, preferred_element_type=jnp.float32) + lax.dot_general(d_raw_half, step_proj, contract_cols, preferred_element_type=jnp.float32)).astype(jnp.bfloat16).reshape(activations.shape)
    grad_in_proj = lax.dot_general(flat_act, d_projected, contract_rows, preferred_element_type=jnp.float32)
    grad_step_proj = lax.dot_general(flat_act, d_raw_half, contract_rows, preferred_element_type=jnp.float32)
    return (layer_out, grad_input, grad_in_proj, grad_step_proj, grad_out_proj_t, grad_conv_kernel, grad_conv_bias, grad_step_bias, grad_decay_rates, grad_skip_gain, grad_norm_gain)
```

```python
import jax
import jax.numpy as jnp
from jax import lax
from jax.experimental import pallas as pl
from jax.experimental.pallas import tpu as pltpu
from jax.sharding import Mesh
from jax.sharding import PartitionSpec as P

SPACE = ("space_0", "space_1", "space_2")
TM = ("tm_0", "tm_1")
TM_SPACE = ("tm_0", "tm_1", "space_0", "space_1", "space_2")
CHIPS = ("tm_0", "tm_1", "space_0", "space_1")
CORE = "space_2"

HIGH = lax.Precision.HIGHEST
NORM_EPS = 1e-05
F32 = jnp.float32
BF16 = jnp.bfloat16
VMEM = pl.BlockSpec(memory_space=pltpu.VMEM)
SMEM = pl.BlockSpec(memory_space=pltpu.SMEM)
LANES = 128


def shape_of(dims, dtype):
    return jax.ShapeDtypeStruct(dims, dtype)


def iota(dims, axis):
    return lax.broadcasted_iota(jnp.int32, dims, axis)


def call(body, out_shape, *args, flops=1 << 20, smem=()):
    specs = [SMEM if k in smem else VMEM for k in range(len(args))]
    outs = jax.tree.map(lambda _: VMEM, out_shape)
    moved = sum(a.size * a.dtype.itemsize for a in args)
    moved += sum(o.size * o.dtype.itemsize for o in jax.tree.leaves(out_shape))
    return pl.pallas_call(
        body,
        out_shape=out_shape,
        in_specs=specs,
        out_specs=outs,
        cost_estimate=pl.CostEstimate(flops=flops, bytes_accessed=moved, transcendentals=0),
    )(*args)


def dot_nt(a, b, precision=None):
    return lax.dot_general(
        a, b, (((1,), (1,)), ((), ())), precision=precision, preferred_element_type=F32
    )


def dot_tn(a, b, precision=None):
    return lax.dot_general(
        a, b, (((0,), (0,)), ((), ())), precision=precision, preferred_element_type=F32
    )


def dot_nn(a, b, precision=None):
    return jnp.dot(a, b, precision=precision, preferred_element_type=F32)


def sigmoid(x):
    return 1.0 / (1.0 + jnp.exp(-x))


def conv_body(low_ref, mid_ref, high_ref, kernel_ref, bias_ref, act_ref, slope_ref):
    rows, cols = mid_ref.shape[:2]
    channels = mid_ref.shape[3]

    def chunk(k, carry):
        lanes = pl.ds(pl.multiple_of(k * LANES, LANES), LANES)
        taps = [kernel_ref[t : t + 1, lanes] for t in range(9)]
        bias = bias_ref[0:1, lanes]
        grid = [
            [low_ref[c, :, lanes].astype(F32) for c in range(cols)],
            *[[mid_ref[r, c, :, lanes].astype(F32) for c in range(cols)] for r in range(rows)],
            [high_ref[c, :, lanes].astype(F32) for c in range(cols)],
        ]
        for r in range(rows):
            for c in range(cols):
                total = None
                for i in range(3):
                    for j in range(3):
                        if 0 <= c + j - 1 < cols:
                            term = taps[3 * i + j] * grid[r + i][c + j - 1]
                            total = term if total is None else total + term
                before = total + bias
                gate = sigmoid(before)
                act_ref[r, c, :, lanes] = (before * gate).astype(BF16)
                slope_ref[r, c, :, lanes] = gate * (1.0 + before * (1.0 - gate))
        return carry

    lax.fori_loop(0, channels // LANES, chunk, 0)


def conv_grad_body(moved_ref, slope_ref, low_ref, mid_ref, high_ref, before_ref, sums_ref):
    rows, cols = mid_ref.shape[:2]
    channels = mid_ref.shape[3]

    def chunk(k, carry):
        lanes = pl.ds(pl.multiple_of(k * LANES, LANES), LANES)
        grid = [
            [low_ref[c, :, lanes].astype(F32) for c in range(cols)],
            *[[mid_ref[r, c, :, lanes].astype(F32) for c in range(cols)] for r in range(rows)],
            [high_ref[c, :, lanes].astype(F32) for c in range(cols)],
        ]
        sums = [None] * 10
        for r in range(rows):
            for c in range(cols):
                d_before = moved_ref[r, c, :, lanes].astype(F32) * slope_ref[r, c, :, lanes]
                before_ref[r, c, :, lanes] = d_before.astype(BF16)
                for i in range(3):
                    for j in range(3):
                        if 0 <= c + j - 1 < cols:
                            term = d_before * grid[r + i][c + j - 1]
                            t = 3 * i + j
                            sums[t] = term if sums[t] is None else sums[t] + term
                sums[9] = d_before if sums[9] is None else sums[9] + d_before
        for t in range(10):
            sums_ref[t : t + 1, lanes] = jnp.sum(sums[t], axis=0, keepdims=True)
        return carry

    lax.fori_loop(0, channels // LANES, chunk, 0)


def conv_spread_body(low_ref, high_ref, moved_ref, slope_ref, kernel_ref, out_ref):
    rows, cols = moved_ref.shape[:2]
    channels = slope_ref.shape[3]

    def chunk(k, carry):
        lanes = pl.ds(pl.multiple_of(k * LANES, LANES), LANES)
        taps = [kernel_ref[t : t + 1, lanes] for t in range(9)]
        grid = [
            [low_ref[c, :, lanes].astype(F32) for c in range(cols)],
            *[
                [
                    moved_ref[r, c, :, lanes].astype(F32) * slope_ref[r, c, :, lanes]
                    for c in range(cols)
                ]
                for r in range(rows)
            ],
            [high_ref[c, :, lanes].astype(F32) for c in range(cols)],
        ]
        for r in range(rows):
            for c in range(cols):
                total = None
                for i in range(3):
                    for j in range(3):
                        if 0 <= c + 1 - j < cols:
                            term = taps[3 * i + j] * grid[r + 2 - i][c + 1 - j]
                            total = term if total is None else total + term
                out_ref[r, c, :, lanes] = total.astype(BF16)
        return carry

    lax.fori_loop(0, channels // LANES, chunk, 0)
    tail = slice(channels, out_ref.shape[3])
    for r in range(rows):
        for c in range(cols):
            out_ref[r, c, :, tail] = moved_ref[r, c, :, tail]


def head_select(heads, width):
    dims = (heads, heads * width)
    return (iota(dims, 1) // width == iota(dims, 0)).astype(F32)


def decay_body(step_ref, rate_ref, decay_ref, weight_ref):
    tokens = step_ref.shape[1]
    frames = step_ref.shape[0] * step_ref.shape[2]
    heads = step_ref.shape[3]
    pairs = heads // 2
    wide = 2 * frames
    place = iota((frames, frames), 0)
    other = iota((frames, frames), 1)
    lower = (place >= other).astype(F32)
    row2 = iota((frames, wide), 0)
    lane2 = iota((frames, wide), 1)
    inner2 = jnp.where(lane2 < frames, lane2, lane2 - frames)
    upper2 = (row2 <= inner2).astype(F32)
    eye2 = (row2 == inner2).astype(F32)
    causal = row2 >= inner2
    first = lax.broadcasted_iota(jnp.int32, (1, wide), 1) < frames
    select = head_select(heads, frames)
    for tok in range(tokens):
        steps = step_ref[:, tok].reshape(frames, heads)
        decay = steps * rate_ref[...]
        running = dot_nn(lower, decay, HIGH)
        running_t = dot_tn(decay, upper2, HIGH)
        steps_t = dot_tn(steps, eye2, HIGH)
        spread_cols = dot_nn(running, select, HIGH)
        for j in range(pairs):
            row = jnp.where(first, running_t[2 * j : 2 * j + 1], running_t[2 * j + 1 : 2 * j + 2])
            step_row = jnp.where(first, steps_t[2 * j : 2 * j + 1], steps_t[2 * j + 1 : 2 * j + 2])
            spread = spread_cols[:, j * wide : (j + 1) * wide] - row
            kept = jnp.where(causal, jnp.exp(-jnp.where(causal, spread, 0.0)), 0.0)
            decay_ref[tok, j] = kept
            weight_ref[tok, j] = kept * step_row


def unpack(tok_values, frames, inner):
    lane = iota((frames, LANES), 1)
    left = lane < LANES // 2
    mixed = tok_values[:, inner : inner + LANES]
    swapped = pltpu.roll(mixed, LANES // 2, 1)
    b_left = jnp.where(left, mixed, 0.0)
    c_left = jnp.where(left, swapped, 0.0)
    b_right = jnp.where(left, 0.0, swapped)
    return left, b_left, c_left, b_right


def score(b_left, c_left):
    both = jnp.concatenate([b_left, b_left], axis=0).astype(BF16)
    return dot_nt(c_left.astype(BF16), both)


def block_diag(pair, left):
    zero = jnp.zeros_like(pair)
    return jnp.concatenate([jnp.where(left, pair, zero), jnp.where(left, zero, pair)], axis=0)


def forward_body(
    act_ref, weight_ref, gate_ref, cot_ref, skip_ref, gain_ref, factor_ref, d_ssd_ref, intra_ref, part_ref
):
    tokens = act_ref.shape[1]
    frames = act_ref.shape[0] * act_ref.shape[2]
    inner = gate_ref.shape[3]
    pairs = weight_ref.shape[1]
    part = None
    for tok in range(tokens):
        values = act_ref[:, tok].astype(F32).reshape(frames, inner + LANES)
        left, b_left, c_left, _ = unpack(values, frames, inner)
        scores = score(b_left, c_left)
        for j in range(pairs):
            lanes = slice(j * LANES, (j + 1) * LANES)
            pair = values[:, lanes]
            mix = (weight_ref[tok, j] * scores).astype(BF16)
            intra_ref[tok, :, lanes] = dot_nn(mix, block_diag(pair, left).astype(BF16))
        ssd = (intra_ref[tok] + skip_ref[...] * values[:, :inner]).astype(BF16).astype(F32)
        gate = gate_ref[:, tok].astype(F32).reshape(frames, inner)
        squashed = sigmoid(gate)
        opened = gate * squashed
        gated = ssd * opened
        scale = lax.rsqrt(jnp.mean(gated * gated, axis=-1, keepdims=True) + NORM_EPS)
        unit = gated * scale
        gain = gain_ref[...]
        cot = cot_ref[:, tok].reshape(frames, inner)
        term = jnp.sum(cot * unit, axis=0, keepdims=True)
        part = term if part is None else part + term
        pulled = cot * gain
        along = jnp.mean(pulled * unit, axis=-1, keepdims=True)
        d_gated = scale * (pulled - unit * along)
        d_ssd_ref[tok] = (d_gated * opened).astype(BF16)
        d_gate = d_gated * ssd * (squashed * (1.0 + gate * (1.0 - squashed)))
        blocks = (act_ref.shape[0], act_ref.shape[2], inner)
        factor_ref[:, tok, :, :inner] = (unit * gain).reshape(blocks).astype(BF16)
        factor_ref[:, tok, :, inner:] = d_gate.reshape(blocks).astype(BF16)
    part_ref[...] = part


def backward_body(
    act_ref,
    decay_ref,
    weight_ref,
    intra_ref,
    d_ssd_ref,
    step_ref,
    raw_ref,
    rate_ref,
    skip_ref,
    out_ref,
    small_ref,
    pulled_ref,
):
    tokens = act_ref.shape[1]
    blocks, per = act_ref.shape[0], act_ref.shape[2]
    frames = blocks * per
    heads = step_ref.shape[3]
    inner = intra_ref.shape[2]
    pairs = heads // 2
    width = inner // heads
    select = head_select(heads, width)
    dims = (frames, frames)
    upper = (iota(dims, 0) <= iota(dims, 1)).astype(F32)
    small = [None, None, None]

    def add(k, term):
        small[k] = term if small[k] is None else small[k] + term

    for tok in range(tokens):
        values = act_ref[:, tok].astype(F32).reshape(frames, inner + LANES)
        left, b_left, c_left, b_right = unpack(values, frames, inner)
        scores = score(b_left, c_left)
        d_scores = jnp.zeros((frames, LANES), F32)
        for j in range(pairs):
            lanes = slice(j * LANES, (j + 1) * LANES)
            pair = values[:, lanes]
            d_pair = d_ssd_ref[tok, :, lanes]
            diag = block_diag(pair, left).astype(BF16)
            d_scores = d_scores + dot_nt(d_pair, diag) * weight_ref[tok, j]
            mix = (decay_ref[tok, j] * scores).astype(BF16)
            wide = dot_tn(mix, d_pair)
            pulled_ref[:, lanes] = jnp.where(left, wide[:frames], wide[frames:])
        u = values[:, :inner]
        dy = d_ssd_ref[tok].astype(F32)
        pulled = pulled_ref[...]
        steps = step_ref[:, tok].reshape(frames, heads)
        rate = rate_ref[...]
        du = dot_nn(steps, select, HIGH) * pulled + skip_ref[...] * dy
        out_ref[:, tok, :, :inner] = du.reshape(blocks, per, inner).astype(BF16)
        q = dot_nt(dy * intra_ref[tok], select, HIGH)
        r = dot_nt(u * pulled, select, HIGH)
        add(2, dot_nt(jnp.sum(dy * u, axis=0, keepdims=True), select, HIGH))
        d_decay = dot_nn(upper, steps * r - q, HIGH)
        add(1, jnp.sum(d_decay * steps, axis=0, keepdims=True))
        d_steps = (r + rate * d_decay).astype(BF16).astype(F32)
        d_raw = d_steps * sigmoid(raw_ref[:, tok].reshape(frames, heads))
        add(0, jnp.sum(d_raw, axis=0, keepdims=True))
        folded = d_scores + pltpu.roll(d_scores, LANES // 2, 1)
        folded = jnp.where(left, folded, 0.0).astype(BF16)
        stacked = jnp.concatenate([b_right, jnp.zeros_like(b_right)], axis=0).astype(BF16)
        d_bc = dot_nn(folded, stacked) + dot_tn(folded, c_left.astype(BF16))[:frames]
        out_ref[:, tok, :, inner : inner + LANES] = d_bc.reshape(blocks, per, LANES).astype(BF16)
        padded = jnp.concatenate([d_raw, jnp.zeros((frames, LANES - heads), F32)], axis=1)
        out_ref[:, tok, :, inner + LANES :] = padded.reshape(blocks, per, LANES).astype(BF16)
    for k in range(3):
        small_ref[k : k + 1, :] = small[k]


def outer_body(core_ref, left_ref, left2_ref, right_ref, right2_ref, out_ref, *, swap):
    rows = left_ref.shape[1]
    cols = right_ref.shape[1]
    groups = out_ref.shape[0]
    core = core_ref[0, 0]
    left_half = rows // swap
    col_half = cols // swap
    step = LANES
    for part in range(swap):
        right = right_ref[:, part * col_half : (part + 1) * col_half]
        right2 = right2_ref[:, part * col_half : (part + 1) * col_half]
        base = (swap - 1 - part) * left_half

        def block(k, carry):
            lanes = pl.ds(pl.multiple_of(base + k * step, step), step)
            total = dot_tn(left_ref[:, lanes], right) + dot_tn(left2_ref[:, lanes], right2)
            split = total.reshape(step // 16, 2, 8, col_half)
            chosen = jnp.where(core == 0, split[:, 0], split[:, 1]).astype(BF16)
            out_ref[pl.ds(k * (step // 16), step // 16), :, part * col_half : (part + 1) * col_half] = chosen
            return carry

        lax.fori_loop(0, groups * 16 // step, block, 0)


def outer(core, left, left2, right, right2, swap):
    groups = left.shape[1] // swap // 16

    def body(*refs):
        outer_body(*refs, swap=swap)

    flops = 4 * left.shape[0] * left.shape[1] // swap * right.shape[1]
    return call(
        body, shape_of((groups, 8, right.shape[1]), BF16), core, left, left2, right, right2, flops=flops, smem=(0,)
    )


def exchange(array, axis):
    return lax.all_to_all(array, axis, split_axis=0, concat_axis=0, tiled=True)


def on_device(
    activations,
    in_proj,
    step_proj,
    step_bias,
    decay_rates,
    conv_kernel,
    conv_bias,
    skip_gain,
    norm_gain,
    out_proj,
    out_cotangent,
):
    frame_count, row_count, col_count, model_width = activations.shape
    inner = out_proj.shape[0]
    heads = step_proj.shape[1]
    channels = conv_bias.shape[0]
    tokens = row_count * col_count
    tm_size = lax.axis_size(TM)
    own = tokens // tm_size
    frames = frame_count * tm_size
    wide = channels + LANES
    grid4 = (row_count, col_count, frame_count)
    tok4 = (tm_size, own, frame_count)
    flat = tokens * frame_count
    core = lax.axis_index(CORE).astype(jnp.int32).reshape(1, 1)
    swap_core = [(0, 1), (1, 0)]
    devices = lax.axis_size(SPACE)
    upward = [(i, i + 1) for i in range(devices - 1)]
    downward = [(b, a) for a, b in upward]

    act = activations.transpose(1, 2, 0, 3).reshape(tokens, frame_count, model_width)
    cot = out_cotangent.transpose(1, 2, 0, 3).reshape(tokens, frame_count, model_width)
    gate_proj, mix_proj = in_proj[:, :inner], in_proj[:, inner:]
    kernel9 = conv_kernel.reshape(9, channels)
    bias1 = conv_bias.reshape(1, channels)

    act_flat = act.reshape(flat, model_width)
    mixed = dot_nn(act_flat, mix_proj).astype(BF16).reshape(*grid4, channels)
    low = lax.ppermute(mixed[row_count - 1], SPACE, upward)
    high = lax.ppermute(mixed[0], SPACE, downward)
    activated, slope = call(
        conv_body,
        (shape_of((*grid4, channels), BF16), shape_of((*grid4, channels), F32)),
        low,
        mixed,
        high,
        kernel9,
        bias1,
    )

    source = exchange(jnp.concatenate([act, cot], axis=-1), TM).reshape(flat, 2 * model_width)
    act_tok, cot_tok = source[:, :model_width], source[:, model_width:]
    gate = dot_nn(act_tok, gate_proj).astype(BF16)
    raw = dot_nn(act_tok, step_proj) + step_bias
    steps = jax.nn.softplus(raw).astype(BF16).astype(F32)
    d_normed = dot_nt(cot_tok, out_proj)
    rate1 = decay_rates.reshape(1, heads)
    skip1 = jnp.repeat(skip_gain, inner // heads).reshape(1, inner)
    gain1 = norm_gain.reshape(1, inner)
    steps4 = steps.reshape(*tok4, heads)
    square = shape_of((own, heads // 2, frames, 2 * frames), F32)
    decay, weight = call(decay_body, (square, square), steps4, rate1)

    moved = exchange(activated.reshape(tokens, frame_count, channels), TM)
    moved = moved.reshape(*tok4, channels)
    factor, d_ssd, intra, norm_part = call(
        forward_body,
        (
            shape_of((*tok4, 2 * inner), BF16),
            shape_of((own, frames, inner), BF16),
            shape_of((own, frames, inner), F32),
            shape_of((1, inner), F32),
        ),
        moved,
        weight,
        gate.reshape(*tok4, inner),
        d_normed.reshape(*tok4, inner),
        skip1,
        gain1,
        flops=1 << 26,
    )
    back = pl.pallas_call(
        backward_body,
        out_shape=(shape_of((*tok4, wide), BF16), shape_of((3, heads), F32)),
        in_specs=[VMEM] * 9,
        out_specs=(VMEM, VMEM),
        scratch_shapes=[pltpu.VMEM((frames, inner), F32)],
        cost_estimate=pl.CostEstimate(flops=1 << 27, bytes_accessed=1 << 22, transcendentals=0),
    )(moved, decay, weight, intra, d_ssd, steps4, raw.reshape(*tok4, heads), rate1, skip1)
    d_moved, small_part = back
    returned = exchange(d_moved.reshape(tokens, frame_count, wide), TM).reshape(*grid4, wide)

    factor_flat = factor.reshape(flat, 2 * inner)
    normed = factor_flat[:, :inner]
    d_gate_tok = factor_flat[:, inner:]
    layer_tok = dot_nn(normed, out_proj).astype(BF16)
    home = exchange(
        jnp.concatenate([layer_tok, d_gate_tok], axis=1).reshape(tokens, frame_count, 2 * inner), TM
    )
    layer_out = home[..., :inner].reshape(*grid4, inner).transpose(2, 0, 1, 3)
    d_gate = home[..., inner:].reshape(flat, inner)
    source2 = lax.ppermute(source, CORE, swap_core)
    factor2 = lax.ppermute(factor_flat, CORE, swap_core)
    early = exchange(outer(core, source, source2, factor_flat, factor2, 2), CHIPS)
    early_sum = jnp.sum(early.astype(F32), axis=0)

    d_before, conv_part = call(
        conv_grad_body,
        (shape_of((*grid4, channels), BF16), shape_of((10, channels), F32)),
        returned,
        slope,
        low,
        mixed,
        high,
    )
    d_low = lax.ppermute(d_before[row_count - 1], SPACE, upward)
    d_high = lax.ppermute(d_before[0], SPACE, downward)
    late_factor = call(
        conv_spread_body,
        shape_of((*grid4, wide), BF16),
        d_low,
        d_high,
        returned,
        slope,
        kernel9,
    ).reshape(flat, wide)
    act2 = lax.ppermute(act_flat, CORE, swap_core)
    late2 = lax.ppermute(late_factor, CORE, swap_core)
    late = exchange(outer(core, act_flat, act2, late_factor, late2, 1), CHIPS)
    late_sum = jnp.sum(late.astype(F32), axis=0)

    back_proj = jnp.concatenate(
        [mix_proj, step_proj, jnp.zeros((model_width, LANES - heads), BF16)], axis=1
    )
    grad_input = (dot_nt(late_factor, back_proj) + dot_nt(d_gate, gate_proj)).astype(BF16)
    grad_input = grad_input.reshape(*grid4, model_width).transpose(2, 0, 1, 3)

    grad_in_proj = jnp.concatenate([early_sum[:, inner:], late_sum[:, :channels]], axis=1)
    grad_step_proj = late_sum[:, channels : channels + heads]
    grad_out_proj_t = early_sum[:, :inner]

    pieces = [conv_part.ravel(), norm_part.ravel(), small_part.ravel()]
    count = lax.axis_size(TM_SPACE)
    size = sum(p.size for p in pieces)
    each = -(-size // (count * LANES)) * LANES
    pieces.append(jnp.zeros((count * each - size,), F32))
    shares = exchange(jnp.concatenate(pieces).reshape(count, 1, each), TM_SPACE)
    share = jnp.sum(shares, axis=0, keepdims=True)
    totals = exchange(jnp.broadcast_to(share, (count, 1, each)), TM_SPACE).ravel()
    at = 9 * channels
    grad_conv_kernel = totals[:at].reshape(3, 3, channels)
    grad_conv_bias = totals[at : at + channels]
    at += channels
    grad_norm_gain = totals[at : at + inner]
    at += inner
    grad_step_bias = totals[at : at + heads]
    grad_decay = totals[at + heads : at + 2 * heads]
    grad_skip = totals[at + 2 * heads : at + 3 * heads]
    return (
        layer_out,
        grad_input,
        grad_in_proj,
        grad_step_proj,
        grad_out_proj_t,
        grad_conv_kernel,
        grad_conv_bias,
        grad_step_bias,
        grad_decay,
        grad_skip,
        grad_norm_gain,
    )


def solution(mesh):
    torus = Mesh(
        mesh.devices.reshape(2, 4, 2, 4, 2), ("tm_0", "tm_1", "space_0", "space_1", "space_2")
    )
    split = P(TM, SPACE, None, None)
    placed = (split, P(), P(), P(), P(), P(), P(), P(), P(), P(), split)
    rows = P(TM_SPACE, None)
    return jax.shard_map(
        on_device,
        mesh=torus,
        in_specs=placed,
        out_specs=(split, split, rows, rows, rows, P(), P(), P(), P(), P(), P()),
        check_vma=False,
    )
```

```python
import jax
import jax.numpy as jnp
from jax import lax
from jax.experimental import pallas as pl
from jax.experimental.pallas import tpu as pltpu
from jax.sharding import Mesh
from jax.sharding import PartitionSpec as P

SPACE = ("space_0", "space_1", "space_2")
TM = ("tm_0", "tm_1")
TM_SPACE = ("tm_0", "tm_1", "space_0", "space_1", "space_2")
CHIPS = ("tm_0", "tm_1", "space_0", "space_1")
CORE = "space_2"

HIGH = lax.Precision.HIGHEST
NORM_EPS = 1e-05
F32 = jnp.float32
BF16 = jnp.bfloat16
VMEM = pl.BlockSpec(memory_space=pltpu.VMEM)
SMEM = pl.BlockSpec(memory_space=pltpu.SMEM)
ANY = pl.BlockSpec(memory_space=pl.ANY)
LANES = 128


def shape_of(dims, dtype):
    return jax.ShapeDtypeStruct(dims, dtype)


def iota(dims, axis):
    return lax.broadcasted_iota(jnp.int32, dims, axis)


def call(body, out_shape, *args, flops=1 << 20, special=None, scratch=(), room=16):
    specs = [(special or {}).get(k, VMEM) for k in range(len(args))]
    outs = jax.tree.map(lambda _: VMEM, out_shape)
    moved = sum(a.size * a.dtype.itemsize for a in args)
    moved += sum(o.size * o.dtype.itemsize for o in jax.tree.leaves(out_shape))
    return pl.pallas_call(
        body,
        out_shape=out_shape,
        in_specs=specs,
        out_specs=outs,
        scratch_shapes=scratch,
        compiler_params=pltpu.CompilerParams(vmem_limit_bytes=room << 20),
        cost_estimate=pl.CostEstimate(flops=flops, bytes_accessed=moved, transcendentals=0),
    )(*args)


def dot_nt(a, b, precision=None):
    return lax.dot_general(
        a, b, (((1,), (1,)), ((), ())), precision=precision, preferred_element_type=F32
    )


def dot_tn(a, b, precision=None):
    return lax.dot_general(
        a, b, (((0,), (0,)), ((), ())), precision=precision, preferred_element_type=F32
    )


def dot_nn(a, b, precision=None):
    return jnp.dot(a, b, precision=precision, preferred_element_type=F32)


def sigmoid(x):
    return 1.0 / (1.0 + jnp.exp(-x))


def conv_body(
    low_ref, mid_ref, high_ref, kernel_ref, bias_ref, act_ref, cot_ref, send_ref, slope_ref
):
    rows, cols = mid_ref.shape[:2]
    channels = mid_ref.shape[3]
    for r in range(rows):
        for c in range(cols):
            send_ref[r, c, :, channels : channels + act_ref.shape[3]] = act_ref[r, c]
            send_ref[r, c, :, channels + act_ref.shape[3] :] = cot_ref[r, c]

    def chunk(k, carry):
        lanes = pl.ds(pl.multiple_of(k * LANES, LANES), LANES)
        taps = [kernel_ref[t : t + 1, lanes] for t in range(9)]
        bias = bias_ref[0:1, lanes]
        grid = [
            [low_ref[c, :, lanes].astype(F32) for c in range(cols)],
            *[[mid_ref[r, c, :, lanes].astype(F32) for c in range(cols)] for r in range(rows)],
            [high_ref[c, :, lanes].astype(F32) for c in range(cols)],
        ]
        for r in range(rows):
            for c in range(cols):
                total = None
                for i in range(3):
                    for j in range(3):
                        if 0 <= c + j - 1 < cols:
                            term = taps[3 * i + j] * grid[r + i][c + j - 1]
                            total = term if total is None else total + term
                before = total + bias
                gate = sigmoid(before)
                send_ref[r, c, :, lanes] = (before * gate).astype(BF16)
                slope_ref[r, c, :, lanes] = gate * (1.0 + before * (1.0 - gate))
        return carry

    lax.fori_loop(0, channels // LANES, chunk, 0)


def conv_grad_body(
    moved_ref, slope_ref, low_ref, mid_ref, high_ref, norm_ref, small_ref, before_ref, sums_ref
):
    rows, cols = mid_ref.shape[:2]
    channels = mid_ref.shape[3]
    heads = small_ref.shape[1]

    def chunk(k, carry):
        lanes = pl.ds(pl.multiple_of(k * LANES, LANES), LANES)
        grid = [
            [low_ref[c, :, lanes].astype(F32) for c in range(cols)],
            *[[mid_ref[r, c, :, lanes].astype(F32) for c in range(cols)] for r in range(rows)],
            [high_ref[c, :, lanes].astype(F32) for c in range(cols)],
        ]
        sums = [None] * 10
        for r in range(rows):
            for c in range(cols):
                d_before = moved_ref[r, c, :, lanes].astype(F32) * slope_ref[r, c, :, lanes]
                before_ref[r, c, :, lanes] = d_before.astype(BF16)
                for i in range(3):
                    for j in range(3):
                        if 0 <= c + j - 1 < cols:
                            term = d_before * grid[r + i][c + j - 1]
                            t = 3 * i + j
                            sums[t] = term if sums[t] is None else sums[t] + term
                sums[9] = d_before if sums[9] is None else sums[9] + d_before
        for t in range(10):
            sums_ref[t : t + 1, lanes] = jnp.sum(sums[t], axis=0, keepdims=True)
        return carry

    lax.fori_loop(0, channels // LANES, chunk, 0)
    inner = norm_ref.shape[1]
    sums_ref[10:11, :inner] = norm_ref[...]
    sums_ref[10:11, inner:] = jnp.zeros((1, channels - inner), F32)
    sums_ref[11:16] = jnp.zeros((5, channels), F32)
    for k in range(3):
        sums_ref[11:12, k * LANES : k * LANES + heads] = small_ref[k : k + 1]


def conv_spread_body(low_ref, high_ref, moved_ref, slope_ref, kernel_ref, out_ref):
    rows, cols = moved_ref.shape[:2]
    channels = slope_ref.shape[3]

    def chunk(k, carry):
        lanes = pl.ds(pl.multiple_of(k * LANES, LANES), LANES)
        taps = [kernel_ref[t : t + 1, lanes] for t in range(9)]
        grid = [
            [low_ref[c, :, lanes].astype(F32) for c in range(cols)],
            *[
                [
                    moved_ref[r, c, :, lanes].astype(F32) * slope_ref[r, c, :, lanes]
                    for c in range(cols)
                ]
                for r in range(rows)
            ],
            [high_ref[c, :, lanes].astype(F32) for c in range(cols)],
        ]
        for r in range(rows):
            for c in range(cols):
                total = None
                for i in range(3):
                    for j in range(3):
                        if 0 <= c + 1 - j < cols:
                            term = taps[3 * i + j] * grid[r + 2 - i][c + 1 - j]
                            total = term if total is None else total + term
                out_ref[r, c, :, lanes] = total.astype(BF16)
        return carry

    lax.fori_loop(0, channels // LANES, chunk, 0)
    tail = slice(channels, out_ref.shape[3])
    for r in range(rows):
        for c in range(cols):
            out_ref[r, c, :, tail] = moved_ref[r, c, :, tail]


def head_select(heads, width):
    dims = (heads, heads * width)
    return (iota(dims, 1) // width == iota(dims, 0)).astype(F32)


def turn_body(core_ref, cot_ref, act_ref, mine_ref, other_ref):
    core = core_ref[0, 0]
    per = cot_ref.shape[1] // LANES
    for k in range(2 * per):
        source = cot_ref if k < per else act_ref
        at = (k % per) * LANES
        block = source[:, at : at + LANES].astype(F32).T
        split = block.reshape(LANES // 16, 2, 8, block.shape[1])
        even = split[:, 0].reshape(LANES // 2, block.shape[1]).astype(BF16)
        odd = split[:, 1].reshape(LANES // 2, block.shape[1]).astype(BF16)
        rows = slice(k * LANES // 2, (k + 1) * LANES // 2)
        mine_ref[rows] = jnp.where(core == 0, even, odd)
        other_ref[rows] = jnp.where(core == 0, odd, even)


def decays(steps, rate, decay_ref, weight_ref, tok):
    frames, heads = steps.shape
    pairs = heads // 2
    wide = 2 * frames
    lower = (iota((frames, frames), 0) >= iota((frames, frames), 1)).astype(F32)
    row2 = iota((frames, wide), 0)
    lane2 = iota((frames, wide), 1)
    inner2 = jnp.where(lane2 < frames, lane2, lane2 - frames)
    upper2 = (row2 <= inner2).astype(F32)
    eye2 = (row2 == inner2).astype(F32)
    causal = row2 >= inner2
    first = iota((1, wide), 1) < frames
    decay = steps * rate
    running = dot_nn(lower, decay, HIGH)
    running_t = dot_tn(decay, upper2, HIGH)
    steps_t = dot_tn(steps, eye2, HIGH)
    spread_cols = dot_nn(running, head_select(heads, frames), HIGH)
    for j in range(pairs):
        row = jnp.where(first, running_t[2 * j : 2 * j + 1], running_t[2 * j + 1 : 2 * j + 2])
        step_row = jnp.where(first, steps_t[2 * j : 2 * j + 1], steps_t[2 * j + 1 : 2 * j + 2])
        spread = spread_cols[:, j * wide : (j + 1) * wide] - row
        kept = jnp.where(causal, jnp.exp(-jnp.where(causal, spread, 0.0)), 0.0)
        decay_ref[tok, j] = kept
        weight_ref[tok, j] = kept * step_row


def unpack(tok_values, frames, inner):
    lane = iota((frames, LANES), 1)
    left = lane < LANES // 2
    mixed = tok_values[:, inner : inner + LANES]
    swapped = pltpu.roll(mixed, LANES // 2, 1)
    b_left = jnp.where(left, mixed, 0.0)
    c_left = jnp.where(left, swapped, 0.0)
    b_right = jnp.where(left, 0.0, swapped)
    return left, b_left, c_left, b_right


def score(b_left, c_left):
    both = jnp.concatenate([b_left, b_left], axis=0).astype(BF16)
    return dot_nt(c_left.astype(BF16), both)


def block_diag(pair, left):
    zero = jnp.zeros_like(pair)
    return jnp.concatenate([jnp.where(left, pair, zero), jnp.where(left, zero, pair)], axis=0)


def rollout_body(
    act_ref,
    rate_ref,
    skip_ref,
    gain_ref,
    step_proj_ref,
    step_bias_ref,
    in_proj_ref,
    out_proj_ref,
    out_ref,
    part_ref,
    small_ref,
    decay_ref,
    weight_ref,
    intra_ref,
    d_ssd_ref,
    pulled_ref,
    gate_proj_ref,
    cot_proj_ref,
    gate_ref,
    cot_ref,
    sems,
):
    fetches = (
        pltpu.make_async_copy(in_proj_ref.at[:, : gate_proj_ref.shape[1]], gate_proj_ref, sems.at[0]),
        pltpu.make_async_copy(out_proj_ref, cot_proj_ref, sems.at[1]),
    )
    for fetch in fetches:
        fetch.start()
    tokens = act_ref.shape[1]
    blocks, per = act_ref.shape[0], act_ref.shape[2]
    frames = blocks * per
    heads = rate_ref.shape[1]
    inner = skip_ref.shape[1]
    pairs = heads // 2
    packed = inner + LANES
    model = out_proj_ref.shape[1]
    at_gate = packed + LANES
    at_cot = at_gate + inner
    select = head_select(heads, inner // heads)
    dims = (frames, frames)
    upper = (iota(dims, 0) <= iota(dims, 1)).astype(F32)
    gain = gain_ref[...]
    rate = rate_ref[...]
    sums = {}

    def add(key, term):
        sums[key] = sums[key] + term if key in sums else term

    def read(tok, start, size):
        return act_ref[:, tok, :, start : start + size].astype(F32).reshape(frames, size)

    def write(tok, start, value):
        size = value.shape[1]
        out_ref[:, tok, :, start : start + size] = value.reshape(blocks, per, size).astype(BF16)

    every = [
        jnp.concatenate(
            [act_ref[:, tok, :, start : start + model].astype(F32).reshape(frames, model) for tok in range(tokens)],
            axis=0,
        ).astype(BF16)
        for start in (packed, packed + model)
    ]
    raw = dot_nn(every[0], step_proj_ref[...]) + step_bias_ref[...]
    small = jnp.exp(-jnp.abs(raw))
    grown = 1.0 + small
    flat = grown == 1.0
    safe = jnp.where(flat, 1.0, grown - 1.0)
    log_part = jnp.where(flat, small, jnp.log(grown) * (small / safe))
    all_steps = (jnp.maximum(raw, 0.0) + log_part).astype(BF16).astype(F32)
    tok_steps = [all_steps[tok * frames : (tok + 1) * frames] for tok in range(tokens)]
    for tok in range(tokens):
        decays(tok_steps[tok], rate, decay_ref, weight_ref, tok)
        values = read(tok, 0, packed)
        left, b_left, c_left, _ = unpack(values, frames, inner)
        scores = score(b_left, c_left)
        for j in range(pairs):
            lanes = slice(j * LANES, (j + 1) * LANES)
            pair = values[:, lanes]
            mix = weight_ref[tok, j] * scores
            coarse = mix.astype(BF16)
            fine = (mix - coarse.astype(F32)).astype(BF16)
            diag = block_diag(pair, left).astype(BF16)
            intra_ref[tok, :, lanes] = dot_nn(coarse, diag) + dot_nn(fine, diag)
    fetches[0].wait()
    gate_ref[...] = dot_nn(every[0], gate_proj_ref[...]).astype(BF16)
    fetches[1].wait()
    cot_ref[...] = dot_nt(every[1], cot_proj_ref[...])

    for tok in range(tokens):
        values = read(tok, 0, inner)
        rows = slice(tok * frames, (tok + 1) * frames)
        ssd = (intra_ref[tok] + skip_ref[...] * values).astype(BF16).astype(F32)
        gate = gate_ref[rows].astype(F32)
        squashed = sigmoid(gate)
        opened = gate * squashed
        gated = ssd * opened
        scale = lax.rsqrt(jnp.mean(gated * gated, axis=-1, keepdims=True) + NORM_EPS)
        unit = gated * scale
        cot = cot_ref[rows]
        add("norm", jnp.sum(cot * unit, axis=0, keepdims=True))
        pulled = cot * gain
        along = jnp.mean(pulled * unit, axis=-1, keepdims=True)
        d_gated = scale * (pulled - unit * along)
        d_ssd_ref[tok] = (d_gated * opened).astype(BF16)
        write(tok, at_gate, unit * gain)
        write(tok, at_cot, d_gated * ssd * (squashed * (1.0 + gate * (1.0 - squashed))))
    part_ref[...] = sums["norm"]

    for tok in range(tokens):
        values = read(tok, 0, packed)
        left, b_left, c_left, b_right = unpack(values, frames, inner)
        scores = score(b_left, c_left)
        d_scores = jnp.zeros((frames, LANES), F32)
        for j in range(pairs):
            lanes = slice(j * LANES, (j + 1) * LANES)
            pair = values[:, lanes]
            d_pair = d_ssd_ref[tok, :, lanes]
            diag = block_diag(pair, left).astype(BF16)
            d_scores = d_scores + dot_nt(d_pair, diag) * weight_ref[tok, j]
            mix = decay_ref[tok, j] * scores
            coarse = mix.astype(BF16)
            fine = (mix - coarse.astype(F32)).astype(BF16)
            wide = dot_tn(coarse, d_pair) + dot_tn(fine, d_pair)
            pulled_ref[:, lanes] = jnp.where(left, wide[:frames], wide[frames:])
        u = values[:, :inner]
        dy = d_ssd_ref[tok].astype(F32)
        pulled = pulled_ref[...]
        steps = tok_steps[tok]
        write(tok, 0, dot_nn(steps, select, HIGH) * pulled + skip_ref[...] * dy)
        q = dot_nt(dy * intra_ref[tok], select, HIGH)
        r = dot_nt(u * pulled, select, HIGH)
        add("skip", dot_nt(jnp.sum(dy * u, axis=0, keepdims=True), select, HIGH))
        d_decay = dot_nn(upper, steps * r - q, HIGH)
        add("rate", jnp.sum(d_decay * steps, axis=0, keepdims=True))
        d_steps = (r + rate * d_decay).astype(BF16).astype(F32)
        d_raw = d_steps * sigmoid(raw[tok * frames : (tok + 1) * frames])
        add("bias", jnp.sum(d_raw, axis=0, keepdims=True))
        folded = d_scores + pltpu.roll(d_scores, LANES // 2, 1)
        folded = jnp.where(left, folded, 0.0).astype(BF16)
        stacked = jnp.concatenate([b_right, jnp.zeros_like(b_right)], axis=0).astype(BF16)
        write(tok, inner, dot_nn(folded, stacked) + dot_tn(folded, c_left.astype(BF16))[:frames])
        write(
            tok,
            packed,
            jnp.concatenate([d_raw, jnp.zeros((frames, LANES - heads), F32)], axis=1),
        )
    for k, key in enumerate(("bias", "rate", "skip")):
        small_ref[k : k + 1, :] = sums[key]


def outer_body(left_ref, left2_ref, home_ref, home2_ref, late_ref, late2_ref, out_ref):
    groups, eight, cols = out_ref.shape
    rows = groups * eight
    width = late_ref.shape[1]
    inner = (cols - width) // 2
    step = 2 * LANES
    parts = (
        (0, home_ref, home2_ref, width, 0, inner),
        (1, home_ref, home2_ref, width + inner, inner, inner),
        (1, late_ref, late2_ref, 0, 2 * inner, width),
    )
    for side, right_ref, right2_ref, start, at, size in parts:
        lanes = slice(start, start + size)
        right = jnp.concatenate([right_ref[:, lanes], right2_ref[:, lanes]], axis=0)
        for k in range(rows // step):
            block = slice(side * rows + k * step, side * rows + (k + 1) * step)
            left = jnp.concatenate([left_ref[block], left2_ref[block]], axis=1)
            total = dot_nn(left, right).reshape(step // eight, eight, size).astype(BF16)
            out_ref[k * step // eight : (k + 1) * step // eight, :, at : at + size] = total


def total_body(share_ref, proj_ref, step_ref, out_ref):
    groups = share_ref.shape[0]
    inner = out_ref.shape[1]
    width = proj_ref.shape[1]
    heads = step_ref.shape[1]
    for k in range(share_ref.shape[2] // LANES):
        lanes = slice(k * LANES, (k + 1) * LANES)
        parts = [share_ref[g, :, lanes].astype(F32) for g in range(groups)]
        while len(parts) > 1:
            parts = [a + b for a, b in zip(parts[::2], parts[1::2])]
        at = k * LANES
        if at < inner:
            out_ref[:, lanes] = parts[0]
        elif at < inner + width:
            proj_ref[:, at - inner : at - inner + LANES] = parts[0]
        else:
            step_ref[...] = parts[0][:, :heads]


def exchange(array, axis):
    return lax.all_to_all(array, axis, split_axis=0, concat_axis=0, tiled=True)


def on_device(
    activations,
    in_proj,
    step_proj,
    step_bias,
    decay_rates,
    conv_kernel,
    conv_bias,
    skip_gain,
    norm_gain,
    out_proj,
    out_cotangent,
):
    frame_count, row_count, col_count, model_width = activations.shape
    inner = out_proj.shape[0]
    heads = step_proj.shape[1]
    channels = conv_bias.shape[0]
    tokens = row_count * col_count
    tm_size = lax.axis_size(TM)
    own = tokens // tm_size
    frames = frame_count * tm_size
    wide = channels + LANES
    grid4 = (row_count, col_count, frame_count)
    tok4 = (tm_size, own, frame_count)
    flat = tokens * frame_count
    core = lax.axis_index(CORE).astype(jnp.int32).reshape(1, 1)
    swap_core = [(0, 1), (1, 0)]
    devices = lax.axis_size(SPACE)
    upward = [(i, i + 1) for i in range(devices - 1)]
    downward = [(b, a) for a, b in upward]

    act = activations.transpose(1, 2, 0, 3).reshape(flat, model_width)
    cot = out_cotangent.transpose(1, 2, 0, 3).reshape(flat, model_width)
    gate_proj, mix_proj = in_proj[:, :inner], in_proj[:, inner:]
    kernel9 = conv_kernel.reshape(9, channels)
    bias1 = conv_bias.reshape(1, channels)
    both = wide + 2 * inner

    mixed = dot_nn(act, mix_proj).astype(BF16).reshape(*grid4, channels)
    low = lax.ppermute(mixed[row_count - 1], SPACE, upward)
    high = lax.ppermute(mixed[0], SPACE, downward)
    send, slope = call(
        conv_body,
        (shape_of((*grid4, channels + 2 * model_width), BF16), shape_of((*grid4, channels), F32)),
        low,
        mixed,
        high,
        kernel9,
        bias1,
        act.reshape(*grid4, model_width),
        cot.reshape(*grid4, model_width),
    )
    moved = exchange(send.reshape(tokens, frame_count, -1), TM).reshape(*tok4, -1)
    half = shape_of((model_width, flat), BF16)
    mine, other = call(turn_body, (half, half), core, cot, act, special={0: SMEM})
    theirs = lax.ppermute(other, CORE, swap_core)

    square = pltpu.VMEM((own, heads // 2, frames, 2 * frames), F32)
    d_moved, norm_part, small_part = call(
        rollout_body,
        (
            shape_of((*tok4, both), BF16),
            shape_of((1, inner), F32),
            shape_of((3, heads), F32),
        ),
        moved,
        decay_rates.reshape(1, heads),
        jnp.repeat(skip_gain, inner // heads).reshape(1, inner),
        norm_gain.reshape(1, inner),
        step_proj,
        step_bias.reshape(1, heads),
        in_proj,
        out_proj,
        special={6: ANY, 7: ANY},
        flops=1 << 29,
        scratch=(
            square,
            square,
            pltpu.VMEM((own, frames, inner), F32),
            pltpu.VMEM((own, frames, inner), BF16),
            pltpu.VMEM((frames, inner), F32),
            pltpu.VMEM((model_width, inner), BF16),
            pltpu.VMEM((inner, model_width), BF16),
            pltpu.VMEM((flat, inner), BF16),
            pltpu.VMEM((flat, inner), F32),
            pltpu.SemaphoreType.DMA((2,)),
        ),
        room=60,
    )
    home = exchange(d_moved.reshape(tokens, frame_count, both), TM)
    returned = home.reshape(*grid4, both)
    home = home.reshape(flat, both)

    d_before, sums = call(
        conv_grad_body,
        (
            shape_of((*grid4, channels), BF16),
            shape_of((16, channels), F32),
        ),
        returned,
        slope,
        low,
        mixed,
        high,
        norm_part,
        small_part,
    )
    d_low = lax.ppermute(d_before[row_count - 1], SPACE, upward)
    d_high = lax.ppermute(d_before[0], SPACE, downward)
    home2 = lax.ppermute(home, CORE, swap_core)
    late = call(
        conv_spread_body, shape_of((*grid4, wide), BF16), d_low, d_high, returned, slope, kernel9
    ).reshape(flat, wide)
    late2 = lax.ppermute(late, CORE, swap_core)
    product = call(
        outer_body,
        shape_of((model_width // 16, 8, both), BF16),
        mine,
        theirs,
        home,
        home2,
        late,
        late2,
        flops=4 * model_width // 2 * both * flat,
    )
    shares = exchange(product, CHIPS)

    sums = sums + lax.ppermute(sums, CORE, swap_core)
    for axis in (("tm_1",), ("space_1",), ("tm_0", "space_0")):
        size = lax.axis_size(axis)
        turns = []
        for k in range(1, size):
            route = [(i, (i + k) % size) for i in range(size)]
            turns.append(lax.ppermute(sums, axis, route))
        sums = (sums + turns[1]) + (turns[0] + turns[2])
    normed = home[:, wide : wide + inner]
    d_gate = home[:, wide + inner :]
    layer = dot_nn(normed, out_proj).astype(BF16)
    grad_input = (
        dot_nt(late[:, :channels], mix_proj)
        + dot_nt(late[:, channels : channels + heads], step_proj)
        + dot_nt(d_gate, gate_proj)
    ).astype(BF16)
    layer_out = layer.reshape(*grid4, model_width).transpose(2, 0, 1, 3)
    grad_input = grad_input.reshape(*grid4, model_width).transpose(2, 0, 1, 3)

    grad_in_proj, grad_step_proj, grad_out_proj_t = call(
        total_body,
        (
            shape_of((8, inner + channels), F32),
            shape_of((8, heads), F32),
            shape_of((8, inner), F32),
        ),
        shares,
    )
    return (
        layer_out,
        grad_input,
        grad_in_proj,
        grad_step_proj,
        grad_out_proj_t,
        sums[:9].reshape(3, 3, channels),
        sums[9],
        sums[11, :heads],
        sums[11, LANES : LANES + heads],
        sums[11, 2 * LANES : 2 * LANES + heads],
        sums[10, :inner],
    )


def solution(mesh):
    torus = Mesh(
        mesh.devices.reshape(2, 4, 2, 4, 2), ("tm_0", "tm_1", "space_0", "space_1", "space_2")
    )
    split = P(TM, SPACE, None, None)
    placed = (split, P(), P(), P(), P(), P(), P(), P(), P(), P(), split)
    rows = P(TM_SPACE, None)

    return jax.shard_map(
        on_device,
        mesh=torus,
        in_specs=placed,
        out_specs=(split, split, rows, rows, rows, P(), P(), P(), P(), P(), P()),
        check_vma=False,
    )
```
